32 devices in a mesh: shard: 2 (over y), rep: 16 (over z, x, core).
Axes of the slice: x: 2, y: 2, z: 4, core: 2. Of those that a mesh axis runs over, the one named last changes fastest.
Arguments:
- layer_in: bfloat16 [32768, 768], P(('shard', 'rep')), may hold values from -6 to 6
- segment_ids: int32 [32, 1024], P(('shard', 'rep')), may hold values from 0 to 2, never falling along the last dimension, each value on 1 to 512 neighbouring positions
- cotangent: bfloat16 [32768, 768], P(('shard', 'rep')), may hold values from -6 to 6
- norm_gain: bfloat16 [768], P('shard'), may hold values from 0.5 to 1.5
- in_weight: bfloat16 [768, 3352], P('shard'), may hold values from -0.21875 to 0.21875
- conv_weight: bfloat16 [4, 1792], P(None, 'shard'), may hold values from -3 to 3
- conv_bias: bfloat16 [1792], P('shard'), may hold values from -0.5 to 0.5
- dt_bias: bfloat16 [24], P('shard'), may hold values from -7 to -3
- a_log: bfloat16 [24], P('shard'), may hold values from 0 to 2.765625
- skip_gain: bfloat16 [24], P('shard'), may hold values from 0.5 to 1.5
- gate_gain: bfloat16 [1536], P('shard'), may hold values from 0.5 to 1.5
- out_weight: bfloat16 [1536, 768], P('shard'), may hold values from -0.15625 to 0.15625
Outputs:
- layer_out: bfloat16 [32768, 768], P(('shard', 'rep'))
- input_grad: bfloat16 [32768, 768], P(('shard', 'rep'))
- norm_gain_grad: float32 [768], P('shard')
- in_weight_grad: float32 [768, 3352], P('shard')
- conv_weight_grad: float32 [4, 1792], P(None, 'shard')
- conv_bias_grad: float32 [1792], P('shard')
- dt_bias_grad: float32 [24], P('shard')
- a_log_grad: float32 [24], P('shard')
- skip_grad: float32 [24], P('shard')
- gate_gain_grad: float32 [1536], P('shard')
- out_weight_grad: float32 [1536, 768], P('shard')
The draws below stay inside these ranges and needn't reach their ends.
Inputs may be any that keep to these rules, and one draw needn't show every extreme that they name: `segment_ids`: within each row the numbers never fall; a document spans 1 to 512 tokens and some document in each row spans exactly that.
All inputs are finite; a program needn't handle non-finite values.
Results may differ from the reference program's by a relative error of at most 0.012.
Values may be sent and summed in bfloat16 or wider, within the bound.
A program may use at most 192 MiB of HBM per device.

```python
import math
import jax
import jax.numpy as jnp
import numpy as np
from jax import lax

D = 768
HEADS = 24
HEADDIM = 64
STATE = 128
CONV = 4
STRETCH = 256
TOK_DEV = 1024
INNER = 1536
XBC = 1792
PROJ = 3352
NSEQ = 32
TOKENS = 32768


def level_of(own_key, extent, shards, low, top_value):
    loudness = 1.0
    for axis_at, shards_of in shards:
        heights = jax.random.uniform(jax.random.fold_in(jax.random.fold_in(own_key, 6), axis_at), (shards_of,), jnp.float32, low / len(shards), top_value / len(shards))
        loudness = loudness * jnp.repeat(jnp.exp(heights), extent[axis_at] // shards_of).reshape((-1,) + (1,) * (len(extent) - 1 - axis_at))
    return loudness


def length_profile(amount, total, most, skew):
    portions = [(1 << 20) // math.isqrt(rank ** skew) + 1 for rank in range(2, amount + 1)]
    surplus, given = total - most - (amount - 1), [1] * (amount - 1)
    while surplus > 0:
        candidates = [i for i in range(amount - 1) if given[i] < most]
        mass, budget = sum([portions[i] for i in candidates]), surplus
        for i in candidates:
            extra = min(most - given[i], max(1, budget * portions[i] // mass), surplus)
            given[i] = given[i] + extra
            surplus = surplus - extra
    return np.array([most] + given)


def ragged_sizes(own_key, amount, total, bound, slope):
    if amount == 2:
        one = jax.random.randint(own_key, (), max(1, total - bound), min(bound, total - 1) + 1)
        return jnp.stack([one, total - one])
    tallies = jnp.asarray(length_profile(amount, total, bound, slope), jnp.int32)
    twos = (amount - 1) // 2
    giver, taker = tallies[1:1 + 2 * twos:2], tallies[2:2 + 2 * twos:2]
    room = jnp.minimum(giver - 1, bound - taker)
    moved = jax.random.randint(jax.random.fold_in(own_key, 1), (twos,), 0, 1 << 20) % (room + 1)
    tallies = tallies.at[1:1 + 2 * twos:2].set(giver - moved).at[2:2 + 2 * twos:2].set(taker + moved)
    return tallies[jax.random.permutation(jax.random.fold_in(own_key, 2), amount)]


def centred(own_key, shape, width, bound, split=(), dtype=jnp.bfloat16):
    values = width * jax.random.normal(own_key, shape, jnp.float32)
    if split:
        values = values * level_of(own_key, shape, split, -0.22, 0.18)
    return jnp.clip(values, -bound, bound).astype(dtype)


def setup_inputs(seed: int = 0) -> dict:
    key_list = jax.random.split(jax.random.key(seed), 13)
    layer_in = centred(key_list[0], (TOKENS, D), 1.0, 6.0, ((0, 32),))
    segment_ids = jax.vmap(lambda own: jnp.searchsorted(jnp.cumsum(ragged_sizes(own, max(3, TOK_DEV // 512), TOK_DEV, TOK_DEV // 2, 1)), jnp.arange(TOK_DEV), side="right"))(jax.random.split(key_list[1], NSEQ)).reshape((NSEQ, TOK_DEV)).astype(jnp.int32)
    cotangent = centred(key_list[2], (TOKENS, D), 1.0, 6.0, ((0, 32),))
    norm_gain = jnp.clip(1.0 + 0.1 * jax.random.normal(key_list[3], (D,), jnp.float32), 0.5, 1.5).astype(jnp.bfloat16)
    in_weight = centred(key_list[4], (D, PROJ), D ** -0.5, 0.21875, ((0, 2),))
    conv_weight = centred(key_list[5], (CONV, XBC), CONV ** -0.5, 3.0, ((1, 2),))
    conv_bias = jnp.clip(jax.random.uniform(key_list[6], (XBC,), jnp.float32, -0.5, 0.5) * level_of(key_list[6], (XBC,), ((0, 2),), -0.4, 0.0), -0.5, 0.5).astype(jnp.bfloat16)
    dt_bias = jnp.clip(-7.0 + 4.0 * jax.random.uniform(key_list[7], (HEADS,), jnp.float32) ** level_of(key_list[7], (HEADS,), ((0, 2),), -0.2, 0.2), -7.0, -3.0).astype(jnp.bfloat16)
    a_log = jnp.clip(2.765625 * jax.random.uniform(key_list[8], (HEADS,), jnp.float32) ** level_of(key_list[8], (HEADS,), ((0, 2),), -0.2, 0.2), 0.0, 2.765625).astype(jnp.bfloat16)
    skip_gain = jnp.clip(0.5 + 1.0 * jax.random.uniform(key_list[9], (HEADS,), jnp.float32) ** level_of(key_list[9], (HEADS,), ((0, 2),), -0.2, 0.2), 0.5, 1.5).astype(jnp.bfloat16)
    gate_gain = jnp.clip(1.0 + 0.1 * jax.random.normal(key_list[10], (INNER,), jnp.float32), 0.5, 1.5).astype(jnp.bfloat16)
    out_weight = centred(key_list[11], (INNER, D), INNER ** -0.5, 0.15625, ((0, 2),))
    return {"layer_in": layer_in, "segment_ids": segment_ids, "cotangent": cotangent, "norm_gain": norm_gain, "in_weight": in_weight, "conv_weight": conv_weight, "conv_bias": conv_bias, "dt_bias": dt_bias, "a_log": a_log, "skip_gain": skip_gain, "gate_gain": gate_gain, "out_weight": out_weight}


eps = 1e-05
highest = lax.Precision.HIGHEST

@jax.custom_vjp
def low(v):
    return lax.optimization_barrier(v.astype(jnp.bfloat16)).astype(jnp.float32)

@jax.custom_vjp
def low_back(v):
    return v

def low_keep(v):
    return (low(v), None)

def low_pass(kept, grad):
    return (grad,)

def back_keep(v):
    return (v, None)

def back_low(kept, grad):
    return (low(grad),)
low.defvjp(low_keep, low_pass)
low_back.defvjp(back_keep, back_low)

def block_step(carry_in, inputs):
    hidden, last_segment = carry_in
    values_flat, b_rows, c_rows, step_t, decay_t, segment = inputs
    length = segment.shape[0]
    values = values_flat.reshape(length, HEADS, HEADDIM)
    running_t = jnp.cumsum(decay_t, axis=1)
    position = jnp.arange(length)
    allowed = (position[:, None] >= position[None, :]) & (segment[:, None] == segment[None, :])
    spread_log = jnp.where(allowed[None], running_t[:, :, None] - running_t[:, None, :], -1e+30)
    kernel = jnp.exp(spread_log)
    pair_scores = jnp.dot(c_rows, b_rows.T, precision=highest)
    weighted = values * step_t.T[:, :, None]
    local_part = jnp.einsum('hts,shp->thp', kernel * pair_scores[None], weighted, precision=highest)
    keep_in = (segment == last_segment).astype(jnp.float32)
    entering = jnp.exp(running_t) * keep_in[None, :]
    carried_part = jnp.einsum('tn,hpn->thp', c_rows, hidden, precision=highest) * entering.T[:, :, None]
    keep_end = (segment == segment[-1]).astype(jnp.float32)
    leaving = jnp.exp(running_t[:, -1:] - running_t) * keep_end[None, :]
    carried = jnp.exp(running_t[:, -1]) * (segment[-1] == last_segment).astype(jnp.float32)
    new_state = hidden * carried[:, None, None] + jnp.einsum('shp,sn->hpn', weighted * leaving.T[:, :, None], b_rows, precision=highest)
    return ((new_state, segment[-1]), (local_part + carried_part).reshape(length, HEADS * HEADDIM))

def state_scan(values, b_rows, c_rows, step_sizes, decay_log, segment):
    length = segment.shape[0]
    blocks = length // STRETCH
    inputs = (values.reshape(blocks, STRETCH, HEADS * HEADDIM), b_rows.reshape(blocks, STRETCH, STATE), c_rows.reshape(blocks, STRETCH, STATE), jnp.transpose(step_sizes.reshape(blocks, STRETCH, HEADS), (0, 2, 1)), jnp.transpose(decay_log.reshape(blocks, STRETCH, HEADS), (0, 2, 1)), segment.reshape(blocks, STRETCH))
    start = (jnp.zeros((HEADS, HEADDIM, STATE), jnp.float32), jnp.array(-1, jnp.int32))
    ending, outputs = lax.scan(jax.checkpoint(block_step), start, inputs)
    return outputs.reshape(length, HEADS, HEADDIM)

def middle(projected, conv_w, conv_b, step_bias, alog, skip, gate_vec, segment):
    length = segment.shape[0]
    gate_part = projected[:, :INNER]
    conv_input = projected[:, INNER:INNER + XBC]
    raw_step = projected[:, INNER + XBC:]
    convolved = jnp.zeros((length, XBC), jnp.float32) + conv_b[None, :]
    for offset in range(CONV):
        shifted = jnp.pad(conv_input, ((offset, 0), (0, 0)))[:length]
        shifted_seg = jnp.pad(segment, (offset, 0), constant_values=-1)[:length]
        same_doc = (shifted_seg == segment).astype(jnp.float32)
        convolved = convolved + conv_w[CONV - 1 - offset][None, :] * shifted * same_doc[:, None]
    active = jax.nn.silu(convolved)
    values = active[:, :INNER].reshape(length, HEADS, HEADDIM)
    b_rows = active[:, INNER:INNER + STATE]
    c_rows = active[:, INNER + STATE:]
    step_sizes = jax.nn.softplus(raw_step + step_bias[None, :])
    decay_log = -jnp.exp(alog)[None, :] * step_sizes
    outputs = state_scan(values, b_rows, c_rows, step_sizes, decay_log, segment) + skip[None, :, None] * values
    gated = outputs.reshape(length, INNER) * jax.nn.silu(gate_part)
    inv_rms = lax.rsqrt(lax.optimization_barrier(jnp.mean(gated * gated, axis=-1, keepdims=True)) + eps)
    return gated * inv_rms * gate_vec[None, :]

def normalize(features, gain_vec):
    inv_rms = lax.rsqrt(lax.optimization_barrier(jnp.mean(features * features, axis=-1, keepdims=True)) + eps)
    return features * inv_rms * gain_vec[None, :]

def whole_layer(features, gain_vec, in_w, conv_w, conv_b, step_bias, alog, skip, gate_vec, out_w, segment):
    normed = low(normalize(features, gain_vec))
    projected = low_back(jnp.dot(normed, in_w, precision=highest))
    mixed = low(middle(projected, conv_w, conv_b, step_bias, alog, skip, gate_vec, segment))
    return features + jnp.dot(mixed, out_w, precision=highest)

def reference(layer_in, segment_ids, cotangent, norm_gain, in_weight, conv_weight, conv_bias, dt_bias, a_log, skip_gain, gate_gain, out_weight):
    params = tuple((p.astype(jnp.float32) for p in (norm_gain, in_weight, conv_weight, conv_bias, dt_bias, a_log, skip_gain, gate_gain, out_weight)))
    inputs = (layer_in.astype(jnp.float32).reshape(NSEQ, TOK_DEV, D), segment_ids, cotangent.astype(jnp.float32).reshape(NSEQ, TOK_DEV, D))

    def per_sequence(totals, sequence):
        features, segment, grad_out = sequence

        def applied(feature_in, *weights):
            return whole_layer(feature_in, *weights, segment)
        result, pullback = jax.vjp(applied, features, *params)
        gradients = pullback(grad_out)
        totals = tuple((a + b for a, b in zip(totals, gradients[1:])))
        return (totals, (result.astype(jnp.bfloat16), gradients[0].astype(jnp.bfloat16)))
    zeros = tuple((jnp.zeros_like(p) for p in params))
    totals, (results, feature_grads) = lax.scan(per_sequence, zeros, inputs)
    averaged = tuple((t / NSEQ for t in totals))
    return (results.reshape(TOKENS, D), feature_grads.reshape(TOKENS, D), averaged[0], averaged[1], averaged[2], averaged[3], averaged[4], averaged[5], averaged[6], averaged[7], averaged[8])
```

```python
import functools

import jax
import jax.numpy as jnp
from jax import lax
from jax.experimental import pallas as pl
from jax.experimental.pallas import tpu as pltpu
from jax.sharding import PartitionSpec as P

HEADS = 24
HEADDIM = 64
STATE = 128
CONV = 4
BLOCK = 128
INNER = 1536
XBC = 1792
WIDE = INNER + XBC
LANES = 128

eps = 1e-05
highest = lax.Precision.HIGHEST
f32 = jnp.float32
bf16 = jnp.bfloat16


def mm(a, b, contract=((1,), (0,))):
    return lax.dot_general(a, b, (contract, ((), ())), preferred_element_type=f32)


def sigmoid(v):
    return 1.0 / (1.0 + jnp.exp(-v))


def softplus(v):
    small = jnp.exp(-jnp.abs(v))
    series = small * (1.0 - small * (0.5 - small * (1.0 / 3.0 - small * 0.25)))
    return jnp.maximum(v, 0.0) + jnp.where(small < 0.03, series, jnp.log(1.0 + small))


def spread(per_head, spread_mat):
    high = per_head.astype(bf16)
    rest = (per_head - high.astype(f32)).astype(bf16)
    return mm(jnp.concatenate([high, rest], axis=1), spread_mat)


def head_sum(per_channel, spread_mat):
    high = per_channel.astype(bf16)
    rest = (per_channel - high.astype(f32)).astype(bf16)
    one = spread_mat[:LANES, :]
    return mm(high, one, ((1,), (1,))) + mm(rest, one, ((1,), (1,)))


def block_terms(raw, aux, seg_row, head_vecs):
    length = raw.shape[0]
    pre = raw + head_vecs[0:1, :]
    step = softplus(pre)
    rate = -jnp.exp(head_vecs[1:2, :])
    decay = rate * step
    row = lax.broadcasted_iota(jnp.int32, (length, length), 0)
    col = lax.broadcasted_iota(jnp.int32, (length, length), 1)
    lower = (row >= col).astype(f32)
    running = lax.dot_general(
        lower, decay, (((1,), (0,)), ((), ())), precision=highest, preferred_element_type=f32
    )
    allowed = (row >= col) & (aux[:, 5:6] == seg_row)
    entering = jnp.exp(running) * aux[:, 3:4]
    leaving = jnp.exp(running[length - 1 : length, :] - running) * aux[:, 4:5]
    return pre, step, rate, decay, running, allowed, entering, leaving, lower


def lane_pair(values, first):
    lane = lax.broadcasted_iota(jnp.int32, values.shape, 1)
    zero = jnp.zeros_like(values)
    return jnp.concatenate(
        [jnp.where(lane < HEADDIM, values, zero), jnp.where(lane >= HEADDIM, values, zero)], axis=0
    )


def spread_of(running, running_t, head):
    diff = running[:, head : head + 1] - running_t[head : head + 1, :]
    return jnp.exp(jnp.minimum(diff, 0.0))


def forward_kernel(
    u_ref, aux_ref, seg_ref, gain_ref, in_ref, step_ref, conv_w_ref, conv_b_ref, head_ref, skip_ref,
    gate_gain_ref, out_w_ref, spread_ref,
    normed_ref, gate_ref, ci_ref, conv_ref, raw_ref, y_ref, state_ref, mixed_ref, out_ref,
    buf, hidden, y_buf,
):
    @pl.when(pl.program_id(0) == 0)
    def _():
        buf[0:8, :] = jnp.zeros((8, XBC), f32)
        hidden[...] = jnp.zeros_like(hidden)

    u = u_ref[...].astype(f32)
    inv = lax.rsqrt(jnp.mean(u * u, axis=-1, keepdims=True) + eps)
    normed = (u * inv * gain_ref[...]).astype(bf16)
    normed_ref[...] = normed
    gate = mm(normed, in_ref[:, :INNER])
    gate_ref[...] = gate
    conv_in = mm(normed, in_ref[:, INNER:WIDE])
    raw = mm(normed, step_ref[...])
    raw_ref[...] = raw
    ci_ref[...] = conv_in.astype(bf16)
    aux = aux_ref[...]
    buf[8 : 8 + BLOCK, :] = conv_in
    conv = conv_b_ref[...] + conv_w_ref[3:4, :] * conv_in
    for k in range(1, CONV):
        conv = conv + conv_w_ref[3 - k : 4 - k, :] * buf[8 - k : 8 - k + BLOCK, :] * aux[:, k - 1 : k]
    buf[0:8, :] = conv_in[BLOCK - 8 :, :]
    conv_ref[...] = conv
    active = conv * sigmoid(conv)
    values = active[:, :INNER]
    b_low = active[:, INNER : INNER + STATE].astype(bf16)
    c_low = active[:, INNER + STATE :].astype(bf16)
    _, step, _, _, running, allowed, entering, leaving, _ = block_terms(
        raw, aux, seg_ref[0], head_ref[...]
    )
    running_t = jnp.transpose(running)
    spread_mat = spread_ref[...]
    weighted = values * spread(step, spread_mat)
    w_low = weighted.astype(bf16)
    scores = jnp.where(allowed, mm(c_low, b_low, ((1,), (1,))), 0.0)
    enter_wide = spread(entering, spread_mat)
    leave_wide = spread(leaving, spread_mat)
    for pair in range(HEADS // 2):
        cols = slice(pair * LANES, (pair + 1) * LANES)
        first = (spread_of(running, running_t, 2 * pair) * scores).astype(bf16)
        second = (spread_of(running, running_t, 2 * pair + 1) * scores).astype(bf16)
        y_buf[:, cols] = mm(
            jnp.concatenate([first, second], axis=1), lane_pair(w_low[:, cols], pair)
        )
    state = hidden[...]
    state_low = state.astype(bf16)
    state_ref[0] = state_low
    y = y_buf[...] + mm(c_low, state_low) * enter_wide + skip_ref[...] * values
    hidden[...] = state * enter_wide[BLOCK - 1 :, :] + mm(
        b_low, (weighted * leave_wide).astype(bf16), ((0,), (0,))
    )
    y_ref[...] = y
    gated = y * (gate * sigmoid(gate))
    inv_g = lax.rsqrt(jnp.mean(gated * gated, axis=-1, keepdims=True) + eps)
    mixed = (gated * inv_g * gate_gain_ref[...]).astype(bf16)
    mixed_ref[...] = mixed
    out_ref[...] = (u + mm(mixed, out_w_ref[...])).astype(bf16)


def backward_kernel(
    u_ref, g_ref, aux_ref, seg_ref, gain_ref, in_ref, step_ref, conv_w_ref, head_ref, skip_ref,
    gate_gain_ref, out_w_ref, spread_ref, gate_ref, ci_ref, conv_ref, raw_ref, y_ref, state_ref,
    ingrad_ref, zx_ref, rawg_ref, dgain_ref, dconv_w_ref, dconv_b_ref, dhead_ref, dskip_ref,
    dgate_gain_ref,
    buf, d_hidden, dw_buf,
):
    @pl.when(pl.program_id(0) == 0)
    def _():
        buf[BLOCK:, :] = jnp.zeros((8, XBC), f32)
        d_hidden[...] = jnp.zeros_like(d_hidden)
        for ref in (dgain_ref, dconv_w_ref, dconv_b_ref, dhead_ref, dskip_ref, dgate_gain_ref):
            ref[...] = jnp.zeros_like(ref)

    def total(v):
        return jnp.sum(v, axis=0, keepdims=True)

    g = g_ref[...]
    aux = aux_ref[...]
    spread_mat = spread_ref[...]
    mixed_grad = mm(g, out_w_ref[...], ((1,), (1,)))
    gate = gate_ref[...]
    y = y_ref[...]
    gate_sig = sigmoid(gate)
    gate_act = gate * gate_sig
    gated = y * gate_act
    inv_g = lax.rsqrt(jnp.mean(gated * gated, axis=-1, keepdims=True) + eps)
    dgate_gain_ref[...] += total(mixed_grad * gated * inv_g)
    scaled = mixed_grad * gate_gain_ref[...]
    mean_term = jnp.mean(scaled * gated, axis=-1, keepdims=True)
    d_gated = inv_g * scaled - gated * (inv_g * inv_g * inv_g * mean_term)
    dy = d_gated * gate_act
    zx_ref[:, :INNER] = (d_gated * y * (gate_sig * (1.0 + gate * (1.0 - gate_sig)))).astype(bf16)

    conv = conv_ref[...]
    conv_sig = sigmoid(conv)
    active = conv * conv_sig
    slope = conv_sig * (1.0 + conv * (1.0 - conv_sig))
    values = active[:, :INNER]
    b_low = active[:, INNER : INNER + STATE].astype(bf16)
    c_low = active[:, INNER + STATE :].astype(bf16)
    pre, step, rate, decay, running, allowed, entering, leaving, lower = block_terms(
        raw_ref[...], aux, seg_ref[0], head_ref[...]
    )
    running_t = jnp.transpose(running)
    step_wide = spread(step, spread_mat)
    weighted = values * step_wide
    w_low = weighted.astype(bf16)
    scores = jnp.where(allowed, mm(c_low, b_low, ((1,), (1,))), 0.0)
    enter_wide = spread(entering, spread_mat)
    leave_wide = spread(leaving, spread_mat)
    dskip_ref[...] += total(dy * values)
    dy_low = dy.astype(bf16)
    d_scores = jnp.zeros((BLOCK, BLOCK), f32)
    d_running = jnp.zeros((BLOCK, LANES), f32)
    half = lax.broadcasted_iota(jnp.int32, (2 * BLOCK, LANES), 0) // BLOCK
    lane = lax.broadcasted_iota(jnp.int32, (2 * BLOCK, LANES), 1)
    for pair in range(HEADS // 2):
        cols = slice(pair * LANES, (pair + 1) * LANES)
        dy_two = lane_pair(dy_low[:, cols], pair)
        d_kernel = mm(dy_two, w_low[:, cols], ((1,), (1,)))
        spread_a = spread_of(running, running_t, 2 * pair)
        spread_b = spread_of(running, running_t, 2 * pair + 1)
        part_a = d_kernel[:BLOCK] * spread_a
        part_b = d_kernel[BLOCK:] * spread_b
        d_scores = d_scores + (part_a + part_b)
        kernel_two = jnp.concatenate(
            [(spread_a * scores).astype(bf16), (spread_b * scores).astype(bf16)], axis=0
        )
        dw_buf[:, cols] = mm(kernel_two, dy_two, ((0,), (0,)))
        flow_a = (part_a * scores).astype(bf16)
        flow_b = (part_b * scores).astype(bf16)
        marks = jnp.where(lane == 2 * pair + half, 1.0, 0.0).astype(bf16)
        d_running = d_running + (
            mm(jnp.concatenate([flow_a, flow_b], axis=1), marks)
            - mm(jnp.concatenate([flow_a, flow_b], axis=0), marks, ((0,), (0,)))
        )
    state_low = state_ref[0]
    d_state = d_hidden[...]
    d_state_low = d_state.astype(bf16)
    entered = dy * enter_wide
    entered_low = entered.astype(bf16)
    d_running = d_running + head_sum(entered * mm(c_low, state_low), spread_mat)
    left = weighted * leave_wide
    left_low = left.astype(bf16)
    d_left = mm(b_low, d_state_low)
    left_flow = head_sum(left * d_left, spread_mat)
    d_running = d_running - left_flow
    carried = enter_wide[BLOCK - 1 :, :]
    carry_row = total(d_state * state_low.astype(f32)) * carried
    carry_flow = head_sum(jnp.broadcast_to(carry_row, (8, INNER)), spread_mat)[0:1, :]
    d_hidden[...] = d_state * carried + mm(c_low, entered_low, ((0,), (0,)))
    d_weighted = dw_buf[...] + d_left * leave_wide
    d_decay = (
        lax.dot_general(
            lower, d_running, (((0,), (0,)), ((), ())), precision=highest, preferred_element_type=f32
        )
        + total(left_flow)
        + carry_flow
    )
    d_step = d_decay * rate + head_sum(d_weighted * values, spread_mat)
    d_raw = d_step * sigmoid(pre)
    dhead_ref[0:1, :] += total(d_raw)
    dhead_ref[1:2, :] += total(d_decay * decay)
    raw_low = d_raw.astype(bf16)
    rawg_ref[...] = raw_low
    d_scores_low = jnp.where(allowed, d_scores, 0.0).astype(bf16)
    d_c = mm(entered_low, state_low, ((1,), (1,))) + mm(d_scores_low, b_low)
    d_b = mm(left_low, d_state_low, ((1,), (1,))) + mm(d_scores_low, c_low, ((0,), (0,)))
    buf[:BLOCK, :INNER] = (dy * skip_ref[...] + d_weighted * step_wide) * slope[:, :INNER]
    buf[:BLOCK, INNER : INNER + STATE] = d_b * slope[:, INNER : INNER + STATE]
    buf[:BLOCK, INNER + STATE :] = d_c * slope[:, INNER + STATE :]
    conv_in = ci_ref[...].astype(f32)
    d_conv = buf[:BLOCK, :]
    dconv_b_ref[...] += total(d_conv)
    dconv_w_ref[3:4, :] += total(conv_in * d_conv)
    d_in = conv_w_ref[3:4, :] * d_conv
    for k in range(1, CONV):
        later = buf[k : BLOCK + k, :] * aux[:, 5 + k : 6 + k]
        d_in = d_in + conv_w_ref[3 - k : 4 - k, :] * later
        dconv_w_ref[3 - k : 4 - k, :] += total(conv_in * later)
    buf[BLOCK:, :] = d_conv[:8, :]
    zx_ref[:, INNER:] = d_in.astype(bf16)
    normed_grad = mm(zx_ref[...], in_ref[:, :WIDE], ((1,), (1,))) + mm(
        raw_low, step_ref[...], ((1,), (1,))
    )
    u = u_ref[...].astype(f32)
    inv = lax.rsqrt(jnp.mean(u * u, axis=-1, keepdims=True) + eps)
    dgain_ref[...] += total(normed_grad * u * inv)
    lifted = normed_grad * gain_ref[...]
    mean_u = jnp.mean(lifted * u, axis=-1, keepdims=True)
    ingrad_ref[...] = (
        g.astype(f32) + inv * lifted - u * (inv * inv * inv * mean_u)
    ).astype(bf16)


def layer(layer_in, segment, cotangent, gain, w_in, conv_w, conv_b, dt_bias, a_log, skip, gate_gain, w_out):
    tokens, width = layer_in.shape
    blocks = tokens // BLOCK
    proj = w_in.shape[1]
    shifted = [jnp.pad(segment, (k, 0), constant_values=-1)[:tokens] for k in range(CONV)]
    after = [jnp.pad(segment, (0, k), constant_values=-1)[k:] for k in range(CONV)]
    by_block = segment.reshape(blocks, BLOCK)
    before = jnp.concatenate([jnp.full((1,), -1, segment.dtype), by_block[:-1, -1]])
    aux = jnp.stack(
        [shifted[k] == segment for k in (1, 2, 3)]
        + [
            (by_block == before[:, None]).reshape(tokens),
            (by_block == by_block[:, -1:]).reshape(tokens),
            segment,
        ]
        + [after[k] == segment for k in (1, 2, 3)]
        + [segment] * 7,
        axis=1,
    ).astype(f32)
    seg_rows = segment.astype(f32).reshape(blocks, 1, BLOCK)
    w_step = jnp.pad(w_in[:, WIDE:], ((0, 0), (0, LANES - HEADS)))
    pad_head = lambda v: jnp.pad(v.astype(f32), (0, LANES - HEADS))
    heads = jnp.stack([pad_head(dt_bias), pad_head(a_log)] + [jnp.zeros((LANES,), f32)] * 6)
    skip_wide = jnp.repeat(skip.astype(f32), HEADDIM).reshape(1, INNER)
    owner = jnp.arange(INNER) // HEADDIM
    one = (jnp.arange(LANES)[:, None] == owner[None, :]).astype(bf16)
    spread_mat = jnp.concatenate([one, one], axis=0)
    gain_row = gain.astype(f32).reshape(1, width)
    conv_w = conv_w.astype(f32)
    conv_b = conv_b.astype(f32).reshape(1, XBC)
    gate_row = gate_gain.astype(f32).reshape(1, INNER)

    def full(a):
        return pl.BlockSpec(a.shape, lambda i: (0,) * a.ndim, pipeline_mode=pl.Buffered(1))

    def rows(cols, order):
        return pl.BlockSpec((BLOCK, cols), lambda i: (order(i), 0))

    fwd = lambda i: i
    bwd = lambda i: blocks - 1 - i
    shape = jax.ShapeDtypeStruct
    params = pltpu.CompilerParams(
        dimension_semantics=("arbitrary",), vmem_limit_bytes=60 * 1024 * 1024
    )
    normed, gate, conv_in, conv, raw, y, states, mixed, layer_out = pl.pallas_call(
        forward_kernel,
        grid=(blocks,),
        in_specs=[
            rows(width, fwd), rows(16, fwd), pl.BlockSpec((1, 1, BLOCK), lambda i: (i, 0, 0)),
            full(gain_row), full(w_in), full(w_step), full(conv_w), full(conv_b), full(heads),
            full(skip_wide), full(gate_row), full(w_out), full(spread_mat),
        ],
        out_specs=[
            rows(width, fwd), rows(INNER, fwd), rows(XBC, fwd), rows(XBC, fwd), rows(LANES, fwd),
            rows(INNER, fwd), pl.BlockSpec((1, STATE, INNER), lambda i: (i, 0, 0)),
            rows(INNER, fwd), rows(width, fwd),
        ],
        out_shape=[
            shape((tokens, width), bf16), shape((tokens, INNER), f32), shape((tokens, XBC), bf16),
            shape((tokens, XBC), f32), shape((tokens, LANES), f32), shape((tokens, INNER), f32),
            shape((blocks, STATE, INNER), bf16), shape((tokens, INNER), bf16),
            shape((tokens, width), bf16),
        ],
        scratch_shapes=[
            pltpu.VMEM((BLOCK + 8, XBC), f32), pltpu.VMEM((STATE, INNER), f32),
            pltpu.VMEM((BLOCK, INNER), f32),
        ],
        compiler_params=params,
        cost_estimate=pl.CostEstimate(
            flops=2 * tokens * width * (proj + INNER) * 2, bytes_accessed=40_000_000,
            transcendentals=tokens * 8000,
        ),
        name="layer_forward",
    )(layer_in, aux, seg_rows, gain_row, w_in, w_step, conv_w, conv_b, heads, skip_wide, gate_row,
      w_out, spread_mat)
    acc = lambda r, c: pl.BlockSpec((r, c), lambda i: (0, 0))
    input_grad, zx_grad, raw_grad, d_gain, d_conv_w, d_conv_b, d_heads, d_skip, d_gate_gain = (
        pl.pallas_call(
            backward_kernel,
            grid=(blocks,),
            in_specs=[
                rows(width, bwd), rows(width, bwd), rows(16, bwd),
                pl.BlockSpec((1, 1, BLOCK), lambda i: (blocks - 1 - i, 0, 0)),
                full(gain_row), full(w_in), full(w_step), full(conv_w), full(heads),
                full(skip_wide), full(gate_row), full(w_out), full(spread_mat),
                rows(INNER, bwd), rows(XBC, bwd), rows(XBC, bwd), rows(LANES, bwd),
                rows(INNER, bwd),
                pl.BlockSpec((1, STATE, INNER), lambda i: (blocks - 1 - i, 0, 0)),
            ],
            out_specs=[
                rows(width, bwd), rows(WIDE, bwd), rows(LANES, bwd), acc(1, width), acc(CONV, XBC),
                acc(1, XBC), acc(8, LANES), acc(1, INNER), acc(1, INNER),
            ],
            out_shape=[
                shape((tokens, width), bf16), shape((tokens, WIDE), bf16),
                shape((tokens, LANES), bf16), shape((1, width), f32), shape((CONV, XBC), f32),
                shape((1, XBC), f32), shape((8, LANES), f32), shape((1, INNER), f32),
                shape((1, INNER), f32),
            ],
            scratch_shapes=[
                pltpu.VMEM((BLOCK + 8, XBC), f32), pltpu.VMEM((STATE, INNER), f32),
                pltpu.VMEM((BLOCK, INNER), f32),
            ],
            compiler_params=params,
            cost_estimate=pl.CostEstimate(
                flops=2 * tokens * width * (proj + INNER) * 3, bytes_accessed=40_000_000,
                transcendentals=tokens * 8000,
            ),
            name="layer_backward",
        )(layer_in, cotangent, aux, seg_rows, gain_row, w_in, w_step, conv_w, heads, skip_wide,
          gate_row, w_out, spread_mat, gate, conv_in, conv, raw, y, states)
    )
    small = (
        d_gain.reshape(width), d_conv_w, d_conv_b.reshape(XBC), d_heads[0, :HEADS],
        d_heads[1, :HEADS], d_skip.reshape(HEADS, HEADDIM).sum(axis=1), d_gate_gain.reshape(INNER),
    )
    return layer_out, input_grad, normed, mixed, zx_grad, raw_grad, small


def own(full, axis):
    count = lax.axis_size("shard")
    size = full.shape[axis] // count
    return lax.dynamic_slice_in_dim(full, lax.axis_index("shard") * size, size, axis)


def body(
    layer_in, segment_ids, cotangent, norm_gain, in_weight, conv_weight, conv_bias, dt_bias, a_log,
    skip_gain, gate_gain, out_weight,
):
    vectors = (norm_gain, conv_weight, conv_bias, dt_bias, a_log, skip_gain, gate_gain)
    packed = jnp.concatenate([v.reshape(-1) for v in vectors])
    packed = lax.all_gather(packed, "shard", axis=0)
    w_in = lax.all_gather(in_weight, "shard", axis=0, tiled=True)
    w_out = lax.all_gather(out_weight, "shard", axis=0, tiled=True)
    whole, at = [], 0
    for v in vectors:
        piece = packed[:, at : at + v.size]
        at += v.size
        if v.ndim == 2:
            piece = piece.reshape((-1,) + v.shape).transpose(1, 0, 2).reshape(v.shape[0], -1)
        else:
            piece = piece.reshape(-1)
        whole.append(piece)
    gain, conv_w, conv_b, step_bias, alog, skip, gate_vec = whole
    layer_out, input_grad, normed, mixed, zx_grad, raw_grad, small = layer(
        layer_in, segment_ids.reshape(-1), cotangent, gain, w_in, conv_w, conv_b, step_bias, alog,
        skip, gate_vec, w_out,
    )
    both = ("shard", "rep")
    factor = 1.0 / (lax.axis_size("shard") * lax.axis_size("rep"))
    out_grad = jnp.einsum("ti,td->id", mixed, cotangent, preferred_element_type=f32).astype(bf16)
    out_sum = lax.psum(lax.psum_scatter(out_grad, "shard", scatter_dimension=0, tiled=True), "rep")
    in_grad = jnp.concatenate(
        [
            jnp.einsum("td,tp->dp", normed, zx_grad, preferred_element_type=f32),
            jnp.einsum("td,tp->dp", normed, raw_grad[:, :HEADS], preferred_element_type=f32),
        ],
        axis=1,
    ).astype(bf16)
    in_sum = lax.psum(lax.psum_scatter(in_grad, "shard", scatter_dimension=0, tiled=True), "rep")
    flat = lax.psum(jnp.concatenate([v.reshape(-1) for v in small]), both) * factor
    outs, at = [], 0
    for v in small:
        piece = flat[at : at + v.size].reshape(v.shape)
        at += v.size
        outs.append(own(piece, v.ndim - 1))
    return (
        layer_out, input_grad, outs[0], in_sum.astype(f32) * factor, outs[1], outs[2], outs[3],
        outs[4], outs[5], outs[6], out_sum.astype(f32) * factor,
    )


def solution(mesh):
    in_specs = (
        P(("shard", "rep"), None),
        P(("shard", "rep"), None),
        P(("shard", "rep"), None),
        P("shard"),
        P("shard", None),
        P(None, "shard"),
        P("shard"),
        P("shard"),
        P("shard"),
        P("shard"),
        P("shard"),
        P("shard", None),
    )
    out_specs = (
        P(("shard", "rep"), None),
        P(("shard", "rep"), None),
        P("shard"),
        P("shard", None),
        P(None, "shard"),
        P("shard"),
        P("shard"),
        P("shard"),
        P("shard"),
        P("shard"),
        P("shard", None),
    )
    return jax.shard_map(body, mesh=mesh, in_specs=in_specs, out_specs=out_specs, check_vma=False)
```

```python
import functools

import jax
import jax.numpy as jnp
from jax import lax
from jax.experimental import pallas as pl
from jax.experimental.pallas import tpu as pltpu
from jax.sharding import PartitionSpec as P

HEADS = 24
HEADDIM = 64
STATE = 128
CONV = 4
BLOCK = 128
INNER = 1536
XBC = 1792
WIDE = INNER + XBC
LANES = 128

eps = 1e-05
highest = lax.Precision.HIGHEST
f32 = jnp.float32
bf16 = jnp.bfloat16


def mm(a, b, contract=((1,), (0,))):
    return lax.dot_general(a, b, (contract, ((), ())), preferred_element_type=f32)


def sigmoid(v):
    return 1.0 / (1.0 + jnp.exp(-v))


def softplus(v):
    small = jnp.exp(-jnp.abs(v))
    series = small * (1.0 - small * (0.5 - small * (1.0 / 3.0 - small * 0.25)))
    return jnp.maximum(v, 0.0) + jnp.where(small < 0.03, series, jnp.log(1.0 + small))


def spread(per_head, spread_mat):
    high = per_head.astype(bf16)
    rest = (per_head - high.astype(f32)).astype(bf16)
    return mm(jnp.concatenate([high, rest], axis=1), spread_mat)


def head_sum(per_channel, spread_mat):
    high = per_channel.astype(bf16)
    rest = (per_channel - high.astype(f32)).astype(bf16)
    one = spread_mat[:LANES, :]
    return mm(high, one, ((1,), (1,))) + mm(rest, one, ((1,), (1,)))


def block_terms(raw, aux, seg_row, head_vecs):
    length = raw.shape[0]
    pre = raw + head_vecs[0:1, :]
    step = softplus(pre)
    rate = -jnp.exp(head_vecs[1:2, :])
    decay = rate * step
    row = lax.broadcasted_iota(jnp.int32, (length, length), 0)
    col = lax.broadcasted_iota(jnp.int32, (length, length), 1)
    lower = (row >= col).astype(f32)
    running = lax.dot_general(
        lower, decay, (((1,), (0,)), ((), ())), precision=highest, preferred_element_type=f32
    )
    allowed = (row >= col) & (aux[:, 5:6] == seg_row)
    entering = jnp.exp(running) * aux[:, 3:4]
    leaving = jnp.exp(running[length - 1 : length, :] - running) * aux[:, 4:5]
    return pre, step, rate, decay, running, allowed, entering, leaving, lower


def lane_pair(values, first):
    lane = lax.broadcasted_iota(jnp.int32, values.shape, 1)
    zero = jnp.zeros_like(values)
    return jnp.concatenate(
        [jnp.where(lane < HEADDIM, values, zero), jnp.where(lane >= HEADDIM, values, zero)], axis=0
    )


def spread_of(running, running_t, head):
    diff = running[:, head : head + 1] - running_t[head : head + 1, :]
    return jnp.exp(jnp.minimum(diff, 0.0))


def forward_kernel(
    u_ref, aux_ref, seg_ref, gain_ref, in_ref, step_ref, conv_w_ref, conv_b_ref, head_ref, skip_ref,
    gate_gain_ref, out_w_ref, spread_ref,
    normed_ref, gate_ref, ci_ref, conv_ref, raw_ref, y_ref, state_ref, mixed_ref, out_ref,
    buf, hidden, y_buf,
):
    @pl.when(pl.program_id(0) == 0)
    def _():
        buf[0:8, :] = jnp.zeros((8, XBC), f32)
        hidden[...] = jnp.zeros_like(hidden)

    u = u_ref[...].astype(f32)
    inv = lax.rsqrt(jnp.mean(u * u, axis=-1, keepdims=True) + eps)
    normed = (u * inv * gain_ref[...]).astype(bf16)
    normed_ref[...] = normed
    gate = mm(normed, in_ref[:, :INNER])
    gate_ref[...] = gate
    conv_in = mm(normed, in_ref[:, INNER:WIDE])
    raw = mm(normed, step_ref[...])
    raw_ref[...] = raw
    ci_ref[...] = conv_in.astype(bf16)
    aux = aux_ref[...]
    buf[8 : 8 + BLOCK, :] = conv_in
    conv = conv_b_ref[...] + conv_w_ref[3:4, :] * conv_in
    for k in range(1, CONV):
        conv = conv + conv_w_ref[3 - k : 4 - k, :] * buf[8 - k : 8 - k + BLOCK, :] * aux[:, k - 1 : k]
    buf[0:8, :] = conv_in[BLOCK - 8 :, :]
    conv_ref[...] = conv
    active = conv * sigmoid(conv)
    values = active[:, :INNER]
    b_low = active[:, INNER : INNER + STATE].astype(bf16)
    c_low = active[:, INNER + STATE :].astype(bf16)
    _, step, _, _, running, allowed, entering, leaving, _ = block_terms(
        raw, aux, seg_ref[0], head_ref[...]
    )
    running_t = jnp.transpose(running)
    spread_mat = spread_ref[...]
    weighted = values * spread(step, spread_mat)
    w_low = weighted.astype(bf16)
    scores = jnp.where(allowed, mm(c_low, b_low, ((1,), (1,))), 0.0)
    enter_wide = spread(entering, spread_mat)
    leave_wide = spread(leaving, spread_mat)
    for pair in range(HEADS // 2):
        cols = slice(pair * LANES, (pair + 1) * LANES)
        first = (spread_of(running, running_t, 2 * pair) * scores).astype(bf16)
        second = (spread_of(running, running_t, 2 * pair + 1) * scores).astype(bf16)
        y_buf[:, cols] = mm(
            jnp.concatenate([first, second], axis=1), lane_pair(w_low[:, cols], pair)
        )
    state = hidden[...]
    state_low = state.astype(bf16)
    state_ref[0] = state_low
    y = y_buf[...] + mm(c_low, state_low) * enter_wide + skip_ref[...] * values
    hidden[...] = state * enter_wide[BLOCK - 1 :, :] + mm(
        b_low, (weighted * leave_wide).astype(bf16), ((0,), (0,))
    )
    y_ref[...] = y
    gated = y * (gate * sigmoid(gate))
    inv_g = lax.rsqrt(jnp.mean(gated * gated, axis=-1, keepdims=True) + eps)
    mixed = (gated * inv_g * gate_gain_ref[...]).astype(bf16)
    mixed_ref[...] = mixed
    out_ref[...] = (u + mm(mixed, out_w_ref[...])).astype(bf16)


def backward_kernel(
    u_ref, g_ref, aux_ref, seg_ref, gain_ref, in_ref, step_ref, conv_w_ref, head_ref, skip_ref,
    gate_gain_ref, out_w_ref, spread_ref, gate_ref, ci_ref, conv_ref, raw_ref, y_ref, state_ref,
    ingrad_ref, zx_ref, rawg_ref, dgain_ref, dconv_w_ref, dconv_b_ref, dhead_ref, dskip_ref,
    dgate_gain_ref,
    buf, d_hidden, dw_buf,
):
    @pl.when(pl.program_id(0) == 0)
    def _():
        buf[BLOCK:, :] = jnp.zeros((8, XBC), f32)
        d_hidden[...] = jnp.zeros_like(d_hidden)
        for ref in (dgain_ref, dconv_w_ref, dconv_b_ref, dhead_ref, dskip_ref, dgate_gain_ref):
            ref[...] = jnp.zeros_like(ref)

    def total(v):
        return jnp.sum(v, axis=0, keepdims=True)

    g = g_ref[...]
    aux = aux_ref[...]
    spread_mat = spread_ref[...]
    mixed_grad = mm(g, out_w_ref[...], ((1,), (1,)))
    gate = gate_ref[...]
    y = y_ref[...]
    gate_sig = sigmoid(gate)
    gate_act = gate * gate_sig
    gated = y * gate_act
    inv_g = lax.rsqrt(jnp.mean(gated * gated, axis=-1, keepdims=True) + eps)
    dgate_gain_ref[...] += total(mixed_grad * gated * inv_g)
    scaled = mixed_grad * gate_gain_ref[...]
    mean_term = jnp.mean(scaled * gated, axis=-1, keepdims=True)
    d_gated = inv_g * scaled - gated * (inv_g * inv_g * inv_g * mean_term)
    dy = d_gated * gate_act
    zx_ref[:, :INNER] = (d_gated * y * (gate_sig * (1.0 + gate * (1.0 - gate_sig)))).astype(bf16)

    conv = conv_ref[...]
    conv_sig = sigmoid(conv)
    active = conv * conv_sig
    slope = conv_sig * (1.0 + conv * (1.0 - conv_sig))
    values = active[:, :INNER]
    b_low = active[:, INNER : INNER + STATE].astype(bf16)
    c_low = active[:, INNER + STATE :].astype(bf16)
    pre, step, rate, decay, running, allowed, entering, leaving, lower = block_terms(
        raw_ref[...], aux, seg_ref[0], head_ref[...]
    )
    running_t = jnp.transpose(running)
    step_wide = spread(step, spread_mat)
    weighted = values * step_wide
    w_low = weighted.astype(bf16)
    scores = jnp.where(allowed, mm(c_low, b_low, ((1,), (1,))), 0.0)
    enter_wide = spread(entering, spread_mat)
    leave_wide = spread(leaving, spread_mat)
    dskip_ref[...] += total(dy * values)
    dy_low = dy.astype(bf16)
    d_scores = jnp.zeros((BLOCK, BLOCK), f32)
    d_running = jnp.zeros((BLOCK, LANES), f32)
    half = lax.broadcasted_iota(jnp.int32, (2 * BLOCK, LANES), 0) // BLOCK
    lane = lax.broadcasted_iota(jnp.int32, (2 * BLOCK, LANES), 1)
    for pair in range(HEADS // 2):
        cols = slice(pair * LANES, (pair + 1) * LANES)
        dy_two = lane_pair(dy_low[:, cols], pair)
        d_kernel = mm(dy_two, w_low[:, cols], ((1,), (1,)))
        spread_a = spread_of(running, running_t, 2 * pair)
        spread_b = spread_of(running, running_t, 2 * pair + 1)
        part_a = d_kernel[:BLOCK] * spread_a
        part_b = d_kernel[BLOCK:] * spread_b
        d_scores = d_scores + (part_a + part_b)
        kernel_two = jnp.concatenate(
            [(spread_a * scores).astype(bf16), (spread_b * scores).astype(bf16)], axis=0
        )
        dw_buf[:, cols] = mm(kernel_two, dy_two, ((0,), (0,)))
        flow_a = (part_a * scores).astype(bf16)
        flow_b = (part_b * scores).astype(bf16)
        marks = jnp.where(lane == 2 * pair + half, 1.0, 0.0).astype(bf16)
        d_running = d_running + (
            mm(jnp.concatenate([flow_a, flow_b], axis=1), marks)
            - mm(jnp.concatenate([flow_a, flow_b], axis=0), marks, ((0,), (0,)))
        )
    state_low = state_ref[0]
    d_state = d_hidden[...]
    d_state_low = d_state.astype(bf16)
    entered = dy * enter_wide
    entered_low = entered.astype(bf16)
    d_running = d_running + head_sum(entered * mm(c_low, state_low), spread_mat)
    left = weighted * leave_wide
    left_low = left.astype(bf16)
    d_left = mm(b_low, d_state_low)
    left_flow = head_sum(left * d_left, spread_mat)
    d_running = d_running - left_flow
    carried = enter_wide[BLOCK - 1 :, :]
    carry_row = total(d_state * state_low.astype(f32)) * carried
    carry_flow = head_sum(jnp.broadcast_to(carry_row, (8, INNER)), spread_mat)[0:1, :]
    d_hidden[...] = d_state * carried + mm(c_low, entered_low, ((0,), (0,)))
    d_weighted = dw_buf[...] + d_left * leave_wide
    d_decay = (
        lax.dot_general(
            lower, d_running, (((0,), (0,)), ((), ())), precision=highest, preferred_element_type=f32
        )
        + total(left_flow)
        + carry_flow
    )
    d_step = d_decay * rate + head_sum(d_weighted * values, spread_mat)
    d_raw = d_step * sigmoid(pre)
    dhead_ref[0:1, :] += total(d_raw)
    dhead_ref[1:2, :] += total(d_decay * decay)
    raw_low = d_raw.astype(bf16)
    rawg_ref[...] = raw_low
    d_scores_low = jnp.where(allowed, d_scores, 0.0).astype(bf16)
    d_c = mm(entered_low, state_low, ((1,), (1,))) + mm(d_scores_low, b_low)
    d_b = mm(left_low, d_state_low, ((1,), (1,))) + mm(d_scores_low, c_low, ((0,), (0,)))
    buf[:BLOCK, :INNER] = (dy * skip_ref[...] + d_weighted * step_wide) * slope[:, :INNER]
    buf[:BLOCK, INNER : INNER + STATE] = d_b * slope[:, INNER : INNER + STATE]
    buf[:BLOCK, INNER + STATE :] = d_c * slope[:, INNER + STATE :]
    conv_in = ci_ref[...].astype(f32)
    d_conv = buf[:BLOCK, :]
    dconv_b_ref[...] += total(d_conv)
    dconv_w_ref[3:4, :] += total(conv_in * d_conv)
    d_in = conv_w_ref[3:4, :] * d_conv
    for k in range(1, CONV):
        later = buf[k : BLOCK + k, :] * aux[:, 5 + k : 6 + k]
        d_in = d_in + conv_w_ref[3 - k : 4 - k, :] * later
        dconv_w_ref[3 - k : 4 - k, :] += total(conv_in * later)
    buf[BLOCK:, :] = d_conv[:8, :]
    zx_ref[:, INNER:] = d_in.astype(bf16)
    normed_grad = mm(zx_ref[...], in_ref[:, :WIDE], ((1,), (1,))) + mm(
        raw_low, step_ref[...], ((1,), (1,))
    )
    u = u_ref[...].astype(f32)
    inv = lax.rsqrt(jnp.mean(u * u, axis=-1, keepdims=True) + eps)
    dgain_ref[...] += total(normed_grad * u * inv)
    lifted = normed_grad * gain_ref[...]
    mean_u = jnp.mean(lifted * u, axis=-1, keepdims=True)
    ingrad_ref[...] = (
        g.astype(f32) + inv * lifted - u * (inv * inv * inv * mean_u)
    ).astype(bf16)


def layer(layer_in, segment, cotangent, gain, w_in, conv_w, conv_b, dt_bias, a_log, skip, gate_gain, w_out):
    tokens, width = layer_in.shape
    blocks = tokens // BLOCK
    proj = w_in.shape[1]
    shifted = [jnp.pad(segment, (k, 0), constant_values=-1)[:tokens] for k in range(CONV)]
    after = [jnp.pad(segment, (0, k), constant_values=-1)[k:] for k in range(CONV)]
    by_block = segment.reshape(blocks, BLOCK)
    before = jnp.concatenate([jnp.full((1,), -1, segment.dtype), by_block[:-1, -1]])
    aux = jnp.stack(
        [shifted[k] == segment for k in (1, 2, 3)]
        + [
            (by_block == before[:, None]).reshape(tokens),
            (by_block == by_block[:, -1:]).reshape(tokens),
            segment,
        ]
        + [after[k] == segment for k in (1, 2, 3)]
        + [segment] * 7,
        axis=1,
    ).astype(f32)
    seg_rows = segment.astype(f32).reshape(blocks, 1, BLOCK)
    w_step = jnp.pad(w_in[:, WIDE:], ((0, 0), (0, LANES - HEADS)))
    pad_head = lambda v: jnp.pad(v.astype(f32), (0, LANES - HEADS))
    heads = jnp.stack([pad_head(dt_bias), pad_head(a_log)] + [jnp.zeros((LANES,), f32)] * 6)
    skip_wide = jnp.repeat(skip.astype(f32), HEADDIM).reshape(1, INNER)
    owner = jnp.arange(INNER) // HEADDIM
    one = (jnp.arange(LANES)[:, None] == owner[None, :]).astype(bf16)
    spread_mat = jnp.concatenate([one, one], axis=0)
    gain_row = gain.astype(f32).reshape(1, width)
    conv_w = conv_w.astype(f32)
    conv_b = conv_b.astype(f32).reshape(1, XBC)
    gate_row = gate_gain.astype(f32).reshape(1, INNER)

    def full(a):
        return pl.BlockSpec(a.shape, lambda i: (0,) * a.ndim, pipeline_mode=pl.Buffered(1))

    def rows(cols, order):
        return pl.BlockSpec((BLOCK, cols), lambda i: (order(i), 0))

    fwd = lambda i: i
    bwd = lambda i: blocks - 1 - i
    shape = jax.ShapeDtypeStruct
    params = pltpu.CompilerParams(
        dimension_semantics=("arbitrary",), vmem_limit_bytes=60 * 1024 * 1024
    )
    normed, gate, conv_in, conv, raw, y, states, mixed, layer_out = pl.pallas_call(
        forward_kernel,
        grid=(blocks,),
        in_specs=[
            rows(width, fwd), rows(16, fwd), pl.BlockSpec((1, 1, BLOCK), lambda i: (i, 0, 0)),
            full(gain_row), full(w_in), full(w_step), full(conv_w), full(conv_b), full(heads),
            full(skip_wide), full(gate_row), full(w_out), full(spread_mat),
        ],
        out_specs=[
            rows(width, fwd), rows(INNER, fwd), rows(XBC, fwd), rows(XBC, fwd), rows(LANES, fwd),
            rows(INNER, fwd), pl.BlockSpec((1, STATE, INNER), lambda i: (i, 0, 0)),
            rows(INNER, fwd), rows(width, fwd),
        ],
        out_shape=[
            shape((tokens, width), bf16), shape((tokens, INNER), f32), shape((tokens, XBC), bf16),
            shape((tokens, XBC), f32), shape((tokens, LANES), f32), shape((tokens, INNER), f32),
            shape((blocks, STATE, INNER), bf16), shape((tokens, INNER), bf16),
            shape((tokens, width), bf16),
        ],
        scratch_shapes=[
            pltpu.VMEM((BLOCK + 8, XBC), f32), pltpu.VMEM((STATE, INNER), f32),
            pltpu.VMEM((BLOCK, INNER), f32),
        ],
        compiler_params=params,
        cost_estimate=pl.CostEstimate(
            flops=2 * tokens * width * (proj + INNER) * 2, bytes_accessed=40_000_000,
            transcendentals=tokens * 8000,
        ),
        name="layer_forward",
    )(layer_in, aux, seg_rows, gain_row, w_in, w_step, conv_w, conv_b, heads, skip_wide, gate_row,
      w_out, spread_mat)
    acc = lambda r, c: pl.BlockSpec((r, c), lambda i: (0, 0))
    input_grad, zx_grad, raw_grad, d_gain, d_conv_w, d_conv_b, d_heads, d_skip, d_gate_gain = (
        pl.pallas_call(
            backward_kernel,
            grid=(blocks,),
            in_specs=[
                rows(width, bwd), rows(width, bwd), rows(16, bwd),
                pl.BlockSpec((1, 1, BLOCK), lambda i: (blocks - 1 - i, 0, 0)),
                full(gain_row), full(w_in), full(w_step), full(conv_w), full(heads),
                full(skip_wide), full(gate_row), full(w_out), full(spread_mat),
                rows(INNER, bwd), rows(XBC, bwd), rows(XBC, bwd), rows(LANES, bwd),
                rows(INNER, bwd),
                pl.BlockSpec((1, STATE, INNER), lambda i: (blocks - 1 - i, 0, 0)),
            ],
            out_specs=[
                rows(width, bwd), rows(WIDE, bwd), rows(LANES, bwd), acc(1, width), acc(CONV, XBC),
                acc(1, XBC), acc(8, LANES), acc(1, INNER), acc(1, INNER),
            ],
            out_shape=[
                shape((tokens, width), bf16), shape((tokens, WIDE), bf16),
                shape((tokens, LANES), bf16), shape((1, width), f32), shape((CONV, XBC), f32),
                shape((1, XBC), f32), shape((8, LANES), f32), shape((1, INNER), f32),
                shape((1, INNER), f32),
            ],
            scratch_shapes=[
                pltpu.VMEM((BLOCK + 8, XBC), f32), pltpu.VMEM((STATE, INNER), f32),
                pltpu.VMEM((BLOCK, INNER), f32),
            ],
            compiler_params=params,
            cost_estimate=pl.CostEstimate(
                flops=2 * tokens * width * (proj + INNER) * 3, bytes_accessed=40_000_000,
                transcendentals=tokens * 8000,
            ),
            name="layer_backward",
        )(layer_in, cotangent, aux, seg_rows, gain_row, w_in, w_step, conv_w, heads, skip_wide,
          gate_row, w_out, spread_mat, gate, conv_in, conv, raw, y, states)
    )
    small = (
        d_gain.reshape(width), d_conv_w, d_conv_b.reshape(XBC), d_heads[0, :HEADS],
        d_heads[1, :HEADS], d_skip.reshape(HEADS, HEADDIM).sum(axis=1), d_gate_gain.reshape(INNER),
    )
    return layer_out, input_grad, normed, mixed, zx_grad, raw_grad, small


PARTS = 3


def gather_kernel(
    w_in_ref, w_out_ref, vec_ref, w_in_full, w_out_full, vec_full, local_sem, send_sem, recv_sem
):
    s, r = lax.axis_index("shard"), lax.axis_index("rep")
    other = 1 - s
    core = r % 2
    side = (r // 2) % 2
    sibling = r + 1 - 2 * core
    beside = r + 2 - 4 * side
    barrier = pltpu.get_barrier_semaphore()
    for target in ((other, r), (s, beside), (s, sibling)):
        pl.semaphore_signal(
            barrier, inc=1, device_id=target, device_id_type=pl.DeviceIdType.MESH
        )
    pl.semaphore_wait(barrier, 3)

    def remote(src, dst, index, target):
        return pltpu.make_async_remote_copy(
            src_ref=src, dst_ref=dst, send_sem=send_sem.at[index], recv_sem=recv_sem.at[index],
            device_id=target, device_id_type=pl.DeviceIdType.MESH,
        )

    vec_rows = vec_ref.shape[0]
    chunks = []
    for part in range(PARTS):
        for src, dst in ((w_in_ref, w_in_full), (w_out_ref, w_out_full)):
            chunks.append((src, dst, src.shape[0] // 4, src.shape[0] // 4 // PARTS, part))
    chunks.sort(key=lambda item: item[0] is w_out_ref)

    def place(chunk, shard, quarter):
        src, _, size, step, part = chunk
        start = shard * src.shape[0] + quarter * size + part * step
        return pl.ds(pl.multiple_of(start, 16), step)

    quarter = r % 4
    beside_quarter = 2 * (1 - side) + core
    first = []
    vec_copy = remote(
        vec_ref, vec_full.at[pl.ds(pl.multiple_of(s * vec_rows, 16), vec_rows), :], 0, (other, r)
    )
    vec_copy.start()
    for n, chunk in enumerate(chunks):
        copy = remote(
            chunk[0].at[place(chunk, 0, quarter), :], chunk[1].at[place(chunk, s, quarter), :],
            1 + 4 * n, (other, r),
        )
        copy.start()
        first.append(copy)
    local = []
    for n, (src, dst) in enumerate(
        ((w_in_ref, w_in_full), (w_out_ref, w_out_full), (vec_ref, vec_full))
    ):
        rows = src.shape[0]
        copy = pltpu.make_async_copy(
            src, dst.at[pl.ds(pl.multiple_of(s * rows, 16), rows), :], local_sem.at[n]
        )
        copy.start()
        local.append(copy)
    second, third = [], []

    def pass_on(n):
        chunk = chunks[n]
        second[n][0].wait_recv()
        where = chunk[1].at[place(chunk, other, beside_quarter), :]
        copy = remote(where, where, 4 + 4 * n, (s, sibling))
        copy.start()
        third.append(copy)

    for n, chunk in enumerate(chunks):
        first[n].wait_recv()
        where = chunk[1].at[place(chunk, other, quarter), :]
        sideways = remote(where, where, 2 + 4 * n, (s, beside))
        sideways.start()
        across = remote(where, where, 3 + 4 * n, (s, sibling))
        across.start()
        second.append((sideways, across))
        if n > 0:
            pass_on(n - 1)
    pass_on(len(chunks) - 1)
    for n in range(len(chunks)):
        second[n][1].wait_recv()
        third[n].wait_recv()
        first[n].wait_send()
        second[n][0].wait_send()
        second[n][1].wait_send()
        third[n].wait_send()
    vec_copy.wait()
    for copy in local:
        copy.wait()


def gather_weights(w_in, w_out, vec):
    count = 1 + 4 * 2 * PARTS
    anywhere = pl.BlockSpec(memory_space=pl.ANY)
    return pl.pallas_call(
        gather_kernel,
        in_specs=[anywhere] * 3,
        out_specs=[anywhere] * 3,
        out_shape=[
            jax.ShapeDtypeStruct((2 * a.shape[0], a.shape[1]), a.dtype) for a in (w_in, w_out, vec)
        ],
        scratch_shapes=[
            pltpu.SemaphoreType.DMA((3,)),
            pltpu.SemaphoreType.DMA((count,)),
            pltpu.SemaphoreType.DMA((count,)),
        ],
        compiler_params=pltpu.CompilerParams(collective_id=0, has_side_effects=True),
        name="gather_weights",
    )(w_in, w_out, vec)


def by_shard(v):
    axis = v.ndim - 1
    cut = v.reshape(v.shape[:axis] + (2, v.shape[axis] // 2))
    return jnp.moveaxis(cut, axis, 0).reshape(2, -1)


def body(
    layer_in, segment_ids, cotangent, norm_gain, in_weight, conv_weight, conv_bias, dt_bias, a_log,
    skip_gain, gate_gain, out_weight,
):
    vectors = (norm_gain, conv_weight, conv_bias, dt_bias, a_log, skip_gain, gate_gain)
    packed = jnp.concatenate([v.reshape(-1) for v in vectors])
    held = packed.size
    packed = jnp.pad(packed, (0, -held % 2048)).reshape(-1, LANES)
    w_in, w_out, packed = gather_weights(in_weight, out_weight, packed)
    packed = packed.reshape(2, -1)
    whole, at = [], 0
    for v in vectors:
        piece = packed[:, at : at + v.size]
        at += v.size
        if v.ndim == 2:
            piece = piece.reshape((-1,) + v.shape).transpose(1, 0, 2).reshape(v.shape[0], -1)
        else:
            piece = piece.reshape(-1)
        whole.append(piece)
    gain, conv_w, conv_b, step_bias, alog, skip, gate_vec = whole
    layer_out, input_grad, normed, mixed, zx_grad, raw_grad, small = layer(
        layer_in, segment_ids.reshape(-1), cotangent, gain, w_in, conv_w, conv_b, step_bias, alog,
        skip, gate_vec, w_out,
    )
    factor = 1.0 / (lax.axis_size("shard") * lax.axis_size("rep"))
    out_grad = jnp.einsum("ti,td->id", mixed, cotangent, preferred_element_type=f32).astype(bf16)
    out_sum = lax.psum(lax.psum_scatter(out_grad, "shard", scatter_dimension=0, tiled=True), "rep")
    in_grad = jnp.concatenate(
        [
            jnp.einsum("td,tp->dp", normed, zx_grad, preferred_element_type=f32).astype(bf16),
            jnp.einsum("td,tp->dp", normed, raw_grad[:, :HEADS], preferred_element_type=f32).astype(
                bf16
            ),
        ],
        axis=1,
    )
    rows, proj = in_weight.shape
    extra = jnp.concatenate([by_shard(v) for v in small], axis=1).astype(bf16)
    held = extra.shape[1]
    extra = jnp.pad(extra, ((0, 0), (0, -held % (16 * proj)))).reshape(2, -1, proj)
    joined = jnp.concatenate([in_grad.reshape(2, rows, proj), extra], axis=1)
    part = lax.psum_scatter(
        joined.reshape(-1, proj), "shard", scatter_dimension=0, tiled=True
    )
    part, out_sum = lax.optimization_barrier((part, out_sum))
    in_sum = lax.psum(part, "rep")
    flat = in_sum[rows:].reshape(-1).astype(f32) * factor
    outs, at = [], 0
    for v in vectors:
        outs.append(flat[at : at + v.size].reshape(v.shape))
        at += v.size
    return (
        layer_out, input_grad, outs[0], in_sum[:rows].astype(f32) * factor, outs[1], outs[2],
        outs[3], outs[4], outs[5], outs[6], out_sum.astype(f32) * factor,
    )


def solution(mesh):
    in_specs = (
        P(("shard", "rep"), None),
        P(("shard", "rep"), None),
        P(("shard", "rep"), None),
        P("shard"),
        P("shard", None),
        P(None, "shard"),
        P("shard"),
        P("shard"),
        P("shard"),
        P("shard"),
        P("shard"),
        P("shard", None),
    )
    out_specs = (
        P(("shard", "rep"), None),
        P(("shard", "rep"), None),
        P("shard"),
        P("shard", None),
        P(None, "shard"),
        P("shard"),
        P("shard"),
        P("shard"),
        P("shard"),
        P("shard"),
        P("shard", None),
    )
    return jax.shard_map(body, mesh=mesh, in_specs=in_specs, out_specs=out_specs, check_vma=False)
```

```python
import functools

import jax
import jax.numpy as jnp
from jax import lax
from jax.experimental import pallas as pl
from jax.experimental.pallas import tpu as pltpu
from jax.sharding import PartitionSpec as P

HEADS = 24
HEADDIM = 64
STATE = 128
CONV = 4
BLOCK = 128
INNER = 1536
XBC = 1792
WIDE = INNER + XBC
LANES = 128

eps = 1e-05
highest = lax.Precision.HIGHEST
f32 = jnp.float32
bf16 = jnp.bfloat16


def mm(a, b, contract=((1,), (0,))):
    return lax.dot_general(a, b, (contract, ((), ())), preferred_element_type=f32)


def sigmoid(v):
    return 1.0 / (1.0 + jnp.exp(-v))


def softplus(v):
    small = jnp.exp(-jnp.abs(v))
    series = small * (1.0 - small * (0.5 - small * (1.0 / 3.0 - small * 0.25)))
    return jnp.maximum(v, 0.0) + jnp.where(small < 0.03, series, jnp.log(1.0 + small))


def spread(per_head, spread_mat):
    high = per_head.astype(bf16)
    rest = (per_head - high.astype(f32)).astype(bf16)
    return mm(jnp.concatenate([high, rest], axis=1), spread_mat)


def head_sum(per_channel, spread_mat):
    high = per_channel.astype(bf16)
    rest = (per_channel - high.astype(f32)).astype(bf16)
    one = spread_mat[:LANES, :]
    return mm(high, one, ((1,), (1,))) + mm(rest, one, ((1,), (1,)))


def block_terms(raw, aux, seg_row, head_vecs):
    length = raw.shape[0]
    pre = raw + head_vecs[0:1, :]
    step = softplus(pre)
    rate = -jnp.exp(head_vecs[1:2, :])
    decay = rate * step
    row = lax.broadcasted_iota(jnp.int32, (length, length), 0)
    col = lax.broadcasted_iota(jnp.int32, (length, length), 1)
    lower = (row >= col).astype(f32)
    running = lax.dot_general(
        lower, decay, (((1,), (0,)), ((), ())), precision=highest, preferred_element_type=f32
    )
    allowed = (row >= col) & (aux[:, 5:6] == seg_row)
    entering = jnp.exp(running) * aux[:, 3:4]
    leaving = jnp.exp(running[length - 1 : length, :] - running) * aux[:, 4:5]
    return pre, step, rate, decay, running, allowed, entering, leaving, lower


def lane_pair(values, first):
    lane = lax.broadcasted_iota(jnp.int32, values.shape, 1)
    zero = jnp.zeros_like(values)
    return jnp.concatenate(
        [jnp.where(lane < HEADDIM, values, zero), jnp.where(lane >= HEADDIM, values, zero)], axis=0
    )


def spread_of(running, running_t, head):
    diff = running[:, head : head + 1] - running_t[head : head + 1, :]
    return jnp.exp(jnp.minimum(diff, 0.0))


def forward_kernel(
    u_ref, g_ref, aux_ref, seg_ref, gain_ref, in_ref, step_ref, conv_w_ref, conv_b_ref, head_ref,
    skip_ref, gate_gain_ref, out_w_ref, spread_ref,
    normed_ref, gate_ref, ci_ref, conv_ref, raw_ref, y_ref, state_ref, mixed_ref, out_ref,
    dgate_gain_ref,
    buf, hidden, y_buf,
):
    @pl.when(pl.program_id(0) == 0)
    def _():
        buf[0:8, :] = jnp.zeros((8, XBC), f32)
        hidden[...] = jnp.zeros_like(hidden)
        dgate_gain_ref[...] = jnp.zeros_like(dgate_gain_ref)

    u = u_ref[...].astype(f32)
    inv = lax.rsqrt(jnp.mean(u * u, axis=-1, keepdims=True) + eps)
    normed = (u * inv * gain_ref[...]).astype(bf16)
    normed_ref[...] = normed
    gate = mm(normed, in_ref[:, :INNER])
    conv_in = mm(normed, in_ref[:, INNER:WIDE])
    raw = mm(normed, step_ref[...])
    raw_ref[...] = raw
    ci_ref[...] = conv_in.astype(bf16)
    aux = aux_ref[...]
    buf[8 : 8 + BLOCK, :] = conv_in
    conv = conv_b_ref[...] + conv_w_ref[3:4, :] * conv_in
    for k in range(1, CONV):
        conv = conv + conv_w_ref[3 - k : 4 - k, :] * buf[8 - k : 8 - k + BLOCK, :] * aux[:, k - 1 : k]
    buf[0:8, :] = conv_in[BLOCK - 8 :, :]
    conv_ref[...] = conv
    active = conv * sigmoid(conv)
    values = active[:, :INNER]
    b_low = active[:, INNER : INNER + STATE].astype(bf16)
    c_low = active[:, INNER + STATE :].astype(bf16)
    _, step, _, _, running, allowed, entering, leaving, _ = block_terms(
        raw, aux, seg_ref[0], head_ref[...]
    )
    running_t = jnp.transpose(running)
    spread_mat = spread_ref[...]
    weighted = values * spread(step, spread_mat)
    w_low = weighted.astype(bf16)
    scores = jnp.where(allowed, mm(c_low, b_low, ((1,), (1,))), 0.0)
    enter_wide = spread(entering, spread_mat)
    leave_wide = spread(leaving, spread_mat)
    for pair in range(HEADS // 2):
        cols = slice(pair * LANES, (pair + 1) * LANES)
        first = (spread_of(running, running_t, 2 * pair) * scores).astype(bf16)
        second = (spread_of(running, running_t, 2 * pair + 1) * scores).astype(bf16)
        y_buf[:, cols] = mm(
            jnp.concatenate([first, second], axis=1), lane_pair(w_low[:, cols], pair)
        )
    state = hidden[...]
    state_low = state.astype(bf16)
    state_ref[0] = state_low
    y = y_buf[...] + mm(c_low, state_low) * enter_wide + skip_ref[...] * values
    hidden[...] = state * enter_wide[BLOCK - 1 :, :] + mm(
        b_low, (weighted * leave_wide).astype(bf16), ((0,), (0,))
    )
    gate_sig = sigmoid(gate)
    gate_act = gate * gate_sig
    gated = y * gate_act
    inv_g = lax.rsqrt(jnp.mean(gated * gated, axis=-1, keepdims=True) + eps)
    mixed = (gated * inv_g * gate_gain_ref[...]).astype(bf16)
    mixed_ref[...] = mixed
    out_ref[...] = (u + mm(mixed, out_w_ref[...])).astype(bf16)
    mixed_grad = mm(g_ref[...], out_w_ref[...], ((1,), (1,)))
    dgate_gain_ref[...] += jnp.sum(mixed_grad * gated * inv_g, axis=0, keepdims=True)
    scaled = mixed_grad * gate_gain_ref[...]
    mean_term = jnp.mean(scaled * gated, axis=-1, keepdims=True)
    d_gated = inv_g * scaled - gated * (inv_g * inv_g * inv_g * mean_term)
    y_ref[...] = d_gated * gate_act
    gate_ref[...] = (d_gated * y * (gate_sig * (1.0 + gate * (1.0 - gate_sig)))).astype(bf16)


def backward_kernel(
    u_ref, g_ref, aux_ref, seg_ref, gain_ref, in_ref, step_ref, conv_w_ref, head_ref, skip_ref,
    spread_ref, gate_ref, ci_ref, conv_ref, raw_ref, y_ref, state_ref,
    ingrad_ref, zx_ref, rawg_ref, dgain_ref, dconv_w_ref, dconv_b_ref, dhead_ref, dskip_ref,
    buf, d_hidden, dw_buf,
):
    @pl.when(pl.program_id(0) == 0)
    def _():
        buf[BLOCK:, :] = jnp.zeros((8, XBC), f32)
        d_hidden[...] = jnp.zeros_like(d_hidden)
        for ref in (dgain_ref, dconv_w_ref, dconv_b_ref, dhead_ref, dskip_ref):
            ref[...] = jnp.zeros_like(ref)

    def total(v):
        return jnp.sum(v, axis=0, keepdims=True)

    g = g_ref[...]
    aux = aux_ref[...]
    spread_mat = spread_ref[...]
    dy = y_ref[...]
    conv = conv_ref[...]
    conv_sig = sigmoid(conv)
    active = conv * conv_sig
    slope = conv_sig * (1.0 + conv * (1.0 - conv_sig))
    values = active[:, :INNER]
    b_low = active[:, INNER : INNER + STATE].astype(bf16)
    c_low = active[:, INNER + STATE :].astype(bf16)
    pre, step, rate, decay, running, allowed, entering, leaving, lower = block_terms(
        raw_ref[...], aux, seg_ref[0], head_ref[...]
    )
    running_t = jnp.transpose(running)
    step_wide = spread(step, spread_mat)
    weighted = values * step_wide
    w_low = weighted.astype(bf16)
    scores = jnp.where(allowed, mm(c_low, b_low, ((1,), (1,))), 0.0)
    enter_wide = spread(entering, spread_mat)
    leave_wide = spread(leaving, spread_mat)
    dskip_ref[...] += total(dy * values)
    dy_low = dy.astype(bf16)
    d_scores = jnp.zeros((BLOCK, BLOCK), f32)
    d_running = jnp.zeros((BLOCK, LANES), f32)
    half = lax.broadcasted_iota(jnp.int32, (2 * BLOCK, LANES), 0) // BLOCK
    lane = lax.broadcasted_iota(jnp.int32, (2 * BLOCK, LANES), 1)
    for pair in range(HEADS // 2):
        cols = slice(pair * LANES, (pair + 1) * LANES)
        dy_two = lane_pair(dy_low[:, cols], pair)
        d_kernel = mm(dy_two, w_low[:, cols], ((1,), (1,)))
        spread_a = spread_of(running, running_t, 2 * pair)
        spread_b = spread_of(running, running_t, 2 * pair + 1)
        part_a = d_kernel[:BLOCK] * spread_a
        part_b = d_kernel[BLOCK:] * spread_b
        d_scores = d_scores + (part_a + part_b)
        kernel_two = jnp.concatenate(
            [(spread_a * scores).astype(bf16), (spread_b * scores).astype(bf16)], axis=0
        )
        dw_buf[:, cols] = mm(kernel_two, dy_two, ((0,), (0,)))
        flow_a = (part_a * scores).astype(bf16)
        flow_b = (part_b * scores).astype(bf16)
        marks = jnp.where(lane == 2 * pair + half, 1.0, 0.0).astype(bf16)
        d_running = d_running + (
            mm(jnp.concatenate([flow_a, flow_b], axis=1), marks)
            - mm(jnp.concatenate([flow_a, flow_b], axis=0), marks, ((0,), (0,)))
        )
    state_low = state_ref[0]
    d_state = d_hidden[...]
    d_state_low = d_state.astype(bf16)
    entered = dy * enter_wide
    entered_low = entered.astype(bf16)
    d_running = d_running + head_sum(entered * mm(c_low, state_low), spread_mat)
    left = weighted * leave_wide
    left_low = left.astype(bf16)
    d_left = mm(b_low, d_state_low)
    left_flow = head_sum(left * d_left, spread_mat)
    d_running = d_running - left_flow
    carried = enter_wide[BLOCK - 1 :, :]
    carry_row = total(d_state * state_low.astype(f32)) * carried
    carry_flow = head_sum(jnp.broadcast_to(carry_row, (8, INNER)), spread_mat)[0:1, :]
    d_hidden[...] = d_state * carried + mm(c_low, entered_low, ((0,), (0,)))
    d_weighted = dw_buf[...] + d_left * leave_wide
    d_decay = (
        lax.dot_general(
            lower, d_running, (((0,), (0,)), ((), ())), precision=highest, preferred_element_type=f32
        )
        + total(left_flow)
        + carry_flow
    )
    d_step = d_decay * rate + head_sum(d_weighted * values, spread_mat)
    d_raw = d_step * sigmoid(pre)
    dhead_ref[0:1, :] += total(d_raw)
    dhead_ref[1:2, :] += total(d_decay * decay)
    raw_low = d_raw.astype(bf16)
    rawg_ref[...] = raw_low
    d_scores_low = jnp.where(allowed, d_scores, 0.0).astype(bf16)
    d_c = mm(entered_low, state_low, ((1,), (1,))) + mm(d_scores_low, b_low)
    d_b = mm(left_low, d_state_low, ((1,), (1,))) + mm(d_scores_low, c_low, ((0,), (0,)))
    buf[:BLOCK, :INNER] = (dy * skip_ref[...] + d_weighted * step_wide) * slope[:, :INNER]
    buf[:BLOCK, INNER : INNER + STATE] = d_b * slope[:, INNER : INNER + STATE]
    buf[:BLOCK, INNER + STATE :] = d_c * slope[:, INNER + STATE :]
    conv_in = ci_ref[...].astype(f32)
    d_conv = buf[:BLOCK, :]
    dconv_b_ref[...] += total(d_conv)
    dconv_w_ref[3:4, :] += total(conv_in * d_conv)
    d_in = conv_w_ref[3:4, :] * d_conv
    for k in range(1, CONV):
        later = buf[k : BLOCK + k, :] * aux[:, 5 + k : 6 + k]
        d_in = d_in + conv_w_ref[3 - k : 4 - k, :] * later
        dconv_w_ref[3 - k : 4 - k, :] += total(conv_in * later)
    buf[BLOCK:, :] = d_conv[:8, :]
    d_in_low = d_in.astype(bf16)
    zx_ref[...] = d_in_low
    normed_grad = (
        mm(gate_ref[...], in_ref[:, :INNER], ((1,), (1,)))
        + mm(d_in_low, in_ref[:, INNER:WIDE], ((1,), (1,)))
        + mm(raw_low, step_ref[...], ((1,), (1,)))
    )
    u = u_ref[...].astype(f32)
    inv = lax.rsqrt(jnp.mean(u * u, axis=-1, keepdims=True) + eps)
    dgain_ref[...] += total(normed_grad * u * inv)
    lifted = normed_grad * gain_ref[...]
    mean_u = jnp.mean(lifted * u, axis=-1, keepdims=True)
    ingrad_ref[...] = (
        g.astype(f32) + inv * lifted - u * (inv * inv * inv * mean_u)
    ).astype(bf16)


def layer(layer_in, segment, cotangent, gain, w_in, conv_w, conv_b, dt_bias, a_log, skip, gate_gain, w_out):
    tokens, width = layer_in.shape
    blocks = tokens // BLOCK
    proj = w_in.shape[1]
    shifted = [jnp.pad(segment, (k, 0), constant_values=-1)[:tokens] for k in range(CONV)]
    after = [jnp.pad(segment, (0, k), constant_values=-1)[k:] for k in range(CONV)]
    by_block = segment.reshape(blocks, BLOCK)
    before = jnp.concatenate([jnp.full((1,), -1, segment.dtype), by_block[:-1, -1]])
    aux = jnp.stack(
        [shifted[k] == segment for k in (1, 2, 3)]
        + [
            (by_block == before[:, None]).reshape(tokens),
            (by_block == by_block[:, -1:]).reshape(tokens),
            segment,
        ]
        + [after[k] == segment for k in (1, 2, 3)]
        + [segment] * 7,
        axis=1,
    ).astype(f32)
    seg_rows = segment.astype(f32).reshape(blocks, 1, BLOCK)
    w_step = jnp.pad(w_in[:, WIDE:], ((0, 0), (0, LANES - HEADS)))
    pad_head = lambda v: jnp.pad(v.astype(f32), (0, LANES - HEADS))
    heads = jnp.stack([pad_head(dt_bias), pad_head(a_log)] + [jnp.zeros((LANES,), f32)] * 6)
    skip_wide = jnp.repeat(skip.astype(f32), HEADDIM).reshape(1, INNER)
    owner = jnp.arange(INNER) // HEADDIM
    one = (jnp.arange(LANES)[:, None] == owner[None, :]).astype(bf16)
    spread_mat = jnp.concatenate([one, one], axis=0)
    gain_row = gain.astype(f32).reshape(1, width)
    conv_w = conv_w.astype(f32)
    conv_b = conv_b.astype(f32).reshape(1, XBC)
    gate_row = gate_gain.astype(f32).reshape(1, INNER)

    def full(a):
        return pl.BlockSpec(a.shape, lambda i: (0,) * a.ndim, pipeline_mode=pl.Buffered(1))

    def rows(cols, order):
        return pl.BlockSpec((BLOCK, cols), lambda i: (order(i), 0))

    fwd = lambda i: i
    bwd = lambda i: blocks - 1 - i
    shape = jax.ShapeDtypeStruct
    params = pltpu.CompilerParams(
        dimension_semantics=("arbitrary",), vmem_limit_bytes=60 * 1024 * 1024
    )
    normed, gate, conv_in, conv, raw, y, states, mixed, layer_out, d_gate_gain = pl.pallas_call(
        forward_kernel,
        grid=(blocks,),
        in_specs=[
            rows(width, fwd), rows(width, fwd), rows(16, fwd), pl.BlockSpec((1, 1, BLOCK), lambda i: (i, 0, 0)),
            full(gain_row), full(w_in), full(w_step), full(conv_w), full(conv_b), full(heads),
            full(skip_wide), full(gate_row), full(w_out), full(spread_mat),
        ],
        out_specs=[
            rows(width, fwd), rows(INNER, fwd), rows(XBC, fwd), rows(XBC, fwd), rows(LANES, fwd),
            rows(INNER, fwd), pl.BlockSpec((1, STATE, INNER), lambda i: (i, 0, 0)),
            rows(INNER, fwd), rows(width, fwd), pl.BlockSpec((1, INNER), lambda i: (0, 0)),
        ],
        out_shape=[
            shape((tokens, width), bf16), shape((tokens, INNER), bf16), shape((tokens, XBC), bf16),
            shape((tokens, XBC), f32), shape((tokens, LANES), f32), shape((tokens, INNER), f32),
            shape((blocks, STATE, INNER), bf16), shape((tokens, INNER), bf16),
            shape((tokens, width), bf16), shape((1, INNER), f32),
        ],
        scratch_shapes=[
            pltpu.VMEM((BLOCK + 8, XBC), f32), pltpu.VMEM((STATE, INNER), f32),
            pltpu.VMEM((BLOCK, INNER), f32),
        ],
        compiler_params=params,
        cost_estimate=pl.CostEstimate(
            flops=2 * tokens * width * (proj + INNER) * 2, bytes_accessed=40_000_000,
            transcendentals=tokens * 8000,
        ),
        name="layer_forward",
    )(layer_in, cotangent, aux, seg_rows, gain_row, w_in, w_step, conv_w, conv_b, heads, skip_wide, gate_row,
      w_out, spread_mat)
    acc = lambda r, c: pl.BlockSpec((r, c), lambda i: (0, 0))
    input_grad, zx_grad, raw_grad, d_gain, d_conv_w, d_conv_b, d_heads, d_skip = (
        pl.pallas_call(
            backward_kernel,
            grid=(blocks,),
            in_specs=[
                rows(width, bwd), rows(width, bwd), rows(16, bwd),
                pl.BlockSpec((1, 1, BLOCK), lambda i: (blocks - 1 - i, 0, 0)),
                full(gain_row), full(w_in), full(w_step), full(conv_w), full(heads),
                full(skip_wide), full(spread_mat),
                rows(INNER, bwd), rows(XBC, bwd), rows(XBC, bwd), rows(LANES, bwd),
                rows(INNER, bwd),
                pl.BlockSpec((1, STATE, INNER), lambda i: (blocks - 1 - i, 0, 0)),
            ],
            out_specs=[
                rows(width, bwd), rows(XBC, bwd), rows(LANES, bwd), acc(1, width), acc(CONV, XBC),
                acc(1, XBC), acc(8, LANES), acc(1, INNER),
            ],
            out_shape=[
                shape((tokens, width), bf16), shape((tokens, XBC), bf16),
                shape((tokens, LANES), bf16), shape((1, width), f32), shape((CONV, XBC), f32),
                shape((1, XBC), f32), shape((8, LANES), f32), shape((1, INNER), f32),
            ],
            scratch_shapes=[
                pltpu.VMEM((BLOCK + 8, XBC), f32), pltpu.VMEM((STATE, INNER), f32),
                pltpu.VMEM((BLOCK, INNER), f32),
            ],
            compiler_params=params,
            cost_estimate=pl.CostEstimate(
                flops=2 * tokens * width * (proj + INNER) * 3, bytes_accessed=40_000_000,
                transcendentals=tokens * 8000,
            ),
            name="layer_backward",
        )(layer_in, cotangent, aux, seg_rows, gain_row, w_in, w_step, conv_w, heads, skip_wide,
          spread_mat, gate, conv_in, conv, raw, y, states)
    )
    small = (
        d_gain.reshape(width), d_conv_w, d_conv_b.reshape(XBC), d_heads[0, :HEADS],
        d_heads[1, :HEADS], d_skip.reshape(HEADS, HEADDIM).sum(axis=1), d_gate_gain.reshape(INNER),
    )
    return layer_out, input_grad, normed, mixed, gate, zx_grad, raw_grad, small


def own(full, axis):
    count = lax.axis_size("shard")
    size = full.shape[axis] // count
    return lax.dynamic_slice_in_dim(full, lax.axis_index("shard") * size, size, axis)


def body(
    layer_in, segment_ids, cotangent, norm_gain, in_weight, conv_weight, conv_bias, dt_bias, a_log,
    skip_gain, gate_gain, out_weight,
):
    vectors = (norm_gain, conv_weight, conv_bias, dt_bias, a_log, skip_gain, gate_gain)
    packed = jnp.concatenate([v.reshape(-1) for v in vectors])
    packed = lax.all_gather(packed, "shard", axis=0)
    w_in = lax.all_gather(in_weight, "shard", axis=0, tiled=True)
    w_out = lax.all_gather(out_weight, "shard", axis=0, tiled=True)
    whole, at = [], 0
    for v in vectors:
        piece = packed[:, at : at + v.size]
        at += v.size
        if v.ndim == 2:
            piece = piece.reshape((-1,) + v.shape).transpose(1, 0, 2).reshape(v.shape[0], -1)
        else:
            piece = piece.reshape(-1)
        whole.append(piece)
    gain, conv_w, conv_b, step_bias, alog, skip, gate_vec = whole
    layer_out, input_grad, normed, mixed, gate_grad, zx_grad, raw_grad, small = layer(
        layer_in, segment_ids.reshape(-1), cotangent, gain, w_in, conv_w, conv_b, step_bias, alog,
        skip, gate_vec, w_out,
    )
    both = ("shard", "rep")
    factor = 1.0 / (lax.axis_size("shard") * lax.axis_size("rep"))
    out_grad = jnp.einsum("ti,td->id", mixed, cotangent, preferred_element_type=f32).astype(bf16)
    early = jnp.einsum("td,tp->dp", normed, gate_grad, preferred_element_type=f32).astype(bf16)
    early, out_sum = lax.psum((early, out_grad), both)
    late = jnp.concatenate(
        [
            jnp.einsum("td,tp->dp", normed, zx_grad, preferred_element_type=f32),
            jnp.einsum("td,tp->dp", normed, raw_grad[:, :HEADS], preferred_element_type=f32),
        ],
        axis=1,
    ).astype(bf16)
    late, early, out_sum = lax.optimization_barrier((late, early, out_sum))
    late = lax.psum(late, both)
    in_sum = jnp.concatenate([own(early, 0), own(late, 0)], axis=1)
    out_sum = own(out_sum, 0)
    flat = lax.psum(jnp.concatenate([v.reshape(-1) for v in small]), both) * factor
    outs, at = [], 0
    for v in small:
        piece = flat[at : at + v.size].reshape(v.shape)
        at += v.size
        outs.append(own(piece, v.ndim - 1))
    return (
        layer_out, input_grad, outs[0], in_sum.astype(f32) * factor, outs[1], outs[2], outs[3],
        outs[4], outs[5], outs[6], out_sum.astype(f32) * factor,
    )


def solution(mesh):
    in_specs = (
        P(("shard", "rep"), None),
        P(("shard", "rep"), None),
        P(("shard", "rep"), None),
        P("shard"),
        P("shard", None),
        P(None, "shard"),
        P("shard"),
        P("shard"),
        P("shard"),
        P("shard"),
        P("shard"),
        P("shard", None),
    )
    out_specs = (
        P(("shard", "rep"), None),
        P(("shard", "rep"), None),
        P("shard"),
        P("shard", None),
        P(None, "shard"),
        P("shard"),
        P("shard"),
        P("shard"),
        P("shard"),
        P("shard"),
        P("shard", None),
    )
    return jax.shard_map(body, mesh=mesh, in_specs=in_specs, out_specs=out_specs, check_vma=False)
```
